32 devices in a mesh: cand: 2 (over x), expert: 16 (over z, y, core).
Axes of the slice: x: 2, y: 2, z: 4, core: 2. Of those that a mesh axis runs over, the one named last changes fastest.
Arguments:
- tokens: bfloat16 [2048, 2048], P('expert'), may hold values from -6 to 6
- targets: bfloat16 [2048, 2048], P('expert'), may hold values from -3 to 3
- routes: int32 [4096, 2], P(('cand', 'expert')), parts along dimension 0, may hold values from 0 to 3, all different within a row; in each aligned block of 128 rows (0 to 127, 128 to 255, ...) at most 80 rows name the same one
- gate_ints: int32 [4096, 2], P(('cand', 'expert')), parts along dimension 0, may hold values from 1 to 4096
- expert_home: int32 [8], P('cand'), parts along dimension 0, may hold values from 0 to 3, each once
- gate_up: bfloat16 [2, 8192, 2048], P(None, ('cand', 'expert')), parts along dimension 1, may hold values from -0.125 to 0.125
- down_master: float32 [8192, 2048], P(('cand', 'expert')), parts along dimension 0, may hold values from -0.1875 to 0.1875
- moment1: float32 [8192, 2048], P(('cand', 'expert')), parts along dimension 0, may hold values from -3 to 3
- moment2: float32 [8192, 2048], P(('cand', 'expert')), parts along dimension 0, may hold values from 0.005 to 0.05
Outputs:
- step_taken: float32 [8192, 2048], P(('cand', 'expert')), parts along dimension 0
- moment1_new: float32 [8192, 2048], P(('cand', 'expert')), parts along dimension 0
The draws below stay inside these ranges and needn't reach their ends.
There are 2 independent parts, one for each index of `cand`. The reference program is written for one: setup_inputs(seed, part) draws one part's arguments, and reference() takes and returns one part's arrays. A program takes and returns all parts, laid end to end along the dimension named above; an argument that names none is the same for every part. Nothing has to cross between parts.
Inputs may be any that keep to these rules, and one draw needn't show every extreme that they name: `routes`: each row names 2 different experts; among the rows of one device no expert is named more than 80 times, a bound that some block reaches. `expert_home`: a permutation of the experts.
All inputs are finite; a program needn't handle non-finite values.
Results may differ from the reference program's by a relative error of at most 0.007.
Values may be sent and summed in bfloat16 or wider, within the bound.
A program may use at most 128 MiB of HBM per device.

```python
import math
import jax
import jax.numpy as jnp
import numpy as np
from jax import lax

D = 2048
FF_W = 1024
TOP = 2
GROUP = 4
TOK_DEV = 128
TOKENS = 2048
EXPERTS = 4
FF_DEV = 256
HIDDEN_ALL = 4096
CAP = 80
N_EXPERT = 16


def with_ends(result, stream_key, low, largest):
    extent = result.shape
    place = [jax.random.randint(jax.random.fold_in(stream_key, axis), (), 0, extent[axis]) for axis in range(len(extent))]
    result = result.at[tuple(place)].set(low)
    longest = extent.index(max(extent))
    place[longest] = (place[longest] + 1) % extent[longest]
    return result.at[tuple(place)].set(largest)


def shard_levels(rng, shape, cuts, smallest, largest):
    factor_of = 1.0
    for position, shards_of in cuts:
        heights = jax.random.uniform(jax.random.fold_in(jax.random.fold_in(rng, 6), position), (shards_of,), jnp.float32, smallest / len(cuts), largest / len(cuts))
        factor_of = factor_of * jnp.repeat(jnp.exp(heights), shape[position] // shards_of).reshape((-1,) + (1,) * (len(shape) - 1 - position))
    return factor_of


def shared_out(own_key, own, number, rows, amount, top, reach, skew):
    ranking = jax.random.permutation(own_key, amount)
    heavy_load, usual = shares(amount, rows * top, reach, skew, True), shares(amount, rows * top, reach, skew, False)
    places = jnp.arange(amount)

    def named(tallies, rotation):
        used = int((tallies > 0).sum())
        fixed = max(1, used // 4)
        shifted = fixed + (places - fixed + rotation * (used - fixed)) % max(1, amount - fixed)
        return jnp.zeros((amount,), jnp.int32).at[ranking[jnp.where(places < fixed, places, shifted)]].set(jnp.asarray(tallies, jnp.int32))

    tallies = jnp.where(number % 4 == 0, named(heavy_load, number // 4), named(usual, number - number // 4 - 1))
    mixed = jax.random.permutation(jax.random.fold_in(own, 3), amount)
    giver, receiver = mixed[0:amount // 2 * 2:2], mixed[1:amount // 2 * 2:2]
    margin = jnp.minimum(tallies[giver] - 1, reach - tallies[receiver]) // 2
    margin = jnp.where((giver == ranking[0]) | (receiver == ranking[0]) | (tallies[receiver] == 0), 0, jnp.maximum(margin, 0))
    shifted = jax.random.randint(jax.random.fold_in(own, 4), (amount // 2,), 0, 1 << 20) % (margin + 1)
    tallies = tallies.at[giver].add(-shifted).at[receiver].add(shifted)
    members = jnp.searchsorted(jnp.cumsum(tallies), jnp.arange(rows * top), side="right").astype(jnp.int32)
    table = members.reshape(top, rows).T
    table = table[jax.random.permutation(jax.random.fold_in(own, 1), rows)]
    rotation = jax.random.randint(jax.random.fold_in(own, 2), (rows, 1), 0, top)
    return jnp.take_along_axis(table, (jnp.arange(top)[None, :] + rotation) % top, axis=1)


def shares(amount, total, bound, skew, full):
    portions = [(1 << 20) // math.isqrt(standing ** skew) + 1 for standing in range(1, amount + 1)]
    largest = bound if full else min(bound, max(-(-total // amount), total * portions[0] // sum(portions)))
    least = 1 if total - largest >= amount - 1 else 0
    holding, surplus = [largest] + [least] * (amount - 1), total - largest - least * (amount - 1)
    while surplus > 0:
        free = [i for i in range(1, amount) if holding[i] < largest] or [i for i in range(1, amount) if holding[i] < bound]
        mass, left = sum([portions[i] for i in free]), surplus
        for i in free:
            more = min(bound - holding[i], max(1, left * portions[i] // mass), surplus)
            holding[i] = holding[i] + more
            surplus = surplus - more
    return np.array(holding)


def bell_draw(rng, shape, width, most, pieces=(), kind=jnp.bfloat16):
    array = width * jax.random.normal(rng, shape, jnp.float32)
    if pieces:
        array = array * shard_levels(rng, shape, pieces, -0.22, 0.18)
    return jnp.clip(array, -most, most).astype(kind)


def setup_inputs(seed: int = 0, part: int = 0) -> dict:
    key_list = jax.random.split(jax.random.key(seed), 10)
    part_splits = jax.random.split(jax.random.fold_in(key_list[9], part), 10)
    tokens = bell_draw(key_list[0], (TOKENS, D), 1.0, 6.0, ((0, 16),))
    targets = bell_draw(key_list[1], (TOKENS, D), 0.5, 3.0, ((0, 16),))
    routes_keys = jax.random.split(jax.random.fold_in(part_splits[2], 1), TOKENS // TOK_DEV)
    routes_turns = jax.random.permutation(jax.random.fold_in(part_splits[2], 3), TOKENS // TOK_DEV)
    routes = jax.vmap(lambda own, number: shared_out(jax.random.fold_in(part_splits[2], 2), own, number, TOK_DEV, EXPERTS, TOP, CAP, 2))(routes_keys, routes_turns).reshape((TOKENS, TOP))
    gate_ints = with_ends(jax.random.randint(part_splits[3], (TOKENS, TOP), 1, 4097), jax.random.fold_in(part_splits[3], 1), 1, 4096).astype(jnp.int32)
    expert_home = jax.random.permutation(part_splits[4], EXPERTS).astype(jnp.int32)
    gate_up = bell_draw(part_splits[5], (2, HIDDEN_ALL, D), D ** -0.5, 0.125, ((1, 16),))
    down_master = bell_draw(part_splits[6], (HIDDEN_ALL, D), FF_W ** -0.5, 0.1875, ((0, 16),), jnp.float32)
    moment1 = bell_draw(part_splits[7], (HIDDEN_ALL, D), 0.5, 3.0, ((0, 16),), jnp.float32)
    moment2 = jnp.clip(jnp.exp(math.log(0.05) - 2.3025851 * jax.random.uniform(part_splits[8], (HIDDEN_ALL, D), jnp.float32) ** shard_levels(part_splits[8], (HIDDEN_ALL, D), ((0, 16),), -0.2, 0.2)), 0.005, 0.05)
    return dict(tokens=tokens, targets=targets, routes=routes, gate_ints=gate_ints, expert_home=expert_home, gate_up=gate_up, down_master=down_master, moment1=moment1, moment2=moment2)


learn_rate = 0.02
epsilon = 1e-08
prior_steps = 20
loss_scale = 0.125

def adam_step(master, moment_one, moment_two, gradient, count):
    moment_one = 0.9 * moment_one + 0.1 * gradient
    moment_two = 0.999 * moment_two + 0.001 * gradient * gradient
    first_fix = 1.0 - 0.9 ** (prior_steps + count)
    second_fix = 1.0 - 0.999 ** (prior_steps + count)
    master = master - learn_rate * (moment_one / first_fix) / (jnp.sqrt(moment_two / second_fix) + epsilon)
    return (master, moment_one, moment_two)

def reference(tokens, targets, routes, gate_ints, expert_home, gate_up, down_master, moment1, moment2):
    slot_count = N_EXPERT * CAP
    flat_ids = routes.reshape(N_EXPERT, TOK_DEV * TOP)
    onehot = (flat_ids[:, :, None] == jnp.arange(EXPERTS, dtype=jnp.int32)[None, None, :]).astype(jnp.int32)
    slot_rank = lax.optimization_barrier(jnp.sum((jnp.cumsum(onehot, axis=1) - onehot) * onehot, axis=2))
    sources = jnp.arange(N_EXPERT, dtype=jnp.int32)[:, None]
    slot_dest = (flat_ids * slot_count + sources * CAP + slot_rank).reshape(-1).astype(jnp.int32)
    token_index = jnp.repeat(jnp.arange(TOKENS, dtype=jnp.int32), TOP)
    weights = gate_ints.reshape(-1).astype(jnp.float32) / 4096.0
    buffer = jnp.zeros((EXPERTS * slot_count, D), jnp.bfloat16).at[slot_dest].set(tokens[token_index])
    buffer = buffer.reshape(EXPERTS, slot_count, D)
    expert_ids = jnp.arange(EXPERTS, dtype=jnp.int32)

    def expert_hidden(inputs):
        expert, arrived = inputs
        row_start = (expert_home[expert] * FF_W).astype(jnp.int32)
        gate_rows = lax.dynamic_slice_in_dim(gate_up[0], row_start, FF_W, 0)
        up_rows = lax.dynamic_slice_in_dim(gate_up[1], row_start, FF_W, 0)
        gate_acts = lax.dot_general(arrived, gate_rows, (((1,), (1,)), ((), ())), preferred_element_type=jnp.float32)
        up_acts = lax.dot_general(arrived, up_rows, (((1,), (1,)), ((), ())), preferred_element_type=jnp.float32)
        return (jax.nn.silu(gate_acts) * up_acts).astype(jnp.bfloat16)
    hiddens = lax.map(expert_hidden, (expert_ids, buffer))

    def expert_output(inputs, master_low):
        expert, hidden = inputs
        row_start = (expert_home[expert] * FF_W).astype(jnp.int32)
        down_rows = lax.dynamic_slice_in_dim(master_low, row_start, FF_W, 0)
        summed = jnp.zeros((slot_count, D), jnp.float32)
        for member in range(GROUP):
            lower_edge = member * FF_DEV
            partial_value = jnp.dot(hidden[:, lower_edge:lower_edge + FF_DEV], down_rows[lower_edge:lower_edge + FF_DEV], preferred_element_type=jnp.float32).astype(jnp.bfloat16)
            summed = summed + partial_value.astype(jnp.float32)
        return summed

    def expert_grad(inputs):
        hidden, grad_rows = inputs
        return lax.dot_general(hidden, grad_rows, (((0,), (0,)), ((), ())), preferred_element_type=jnp.float32)
    master, moment_one, moment_two = (down_master, moment1, moment2)
    for round_index in range(2):
        master_low = master.astype(jnp.bfloat16)
        outputs = lax.map(lambda inputs: expert_output(inputs, master_low), (expert_ids, hiddens))
        picked = outputs.reshape(EXPERTS * slot_count, D)[slot_dest] * weights[:, None]
        mixed = lax.optimization_barrier(jnp.sum(picked.reshape(TOKENS, TOP, D), axis=1))
        residual = (mixed - targets.astype(jnp.float32)) * loss_scale
        grad_slots = (weights[:, None] * residual[token_index]).astype(jnp.bfloat16)
        grad_buffer = jnp.zeros((EXPERTS * slot_count, D), jnp.bfloat16).at[slot_dest].set(grad_slots)
        grads = lax.map(expert_grad, (hiddens, grad_buffer.reshape(EXPERTS, slot_count, D)))
        gradient = jnp.zeros((EXPERTS, FF_W, D), jnp.float32).at[expert_home].set(grads).reshape(HIDDEN_ALL, D)
        master, moment_one, moment_two = adam_step(master, moment_one, moment_two, gradient, round_index + 1)
    return ((down_master - master) / learn_rate, moment_one)
```

```python
import jax
import jax.numpy as jnp
from jax import lax
from jax.sharding import PartitionSpec as P

GROUP = 4


learn_rate = 0.02
epsilon = 1e-08
prior_steps = 20
loss_scale = 0.125


def flipped(block, mask):
    count = lax.axis_size("expert")
    return lax.ppermute(block, "expert", [(i, i ^ mask) for i in range(count)])


def member_gather(block, axis):
    across = flipped(block, 2)
    near = flipped(block, 1)
    far = flipped(across, 1)
    return jnp.concatenate([block, near, across, far], axis=axis)


def feature_slice(block, index, width):
    return lax.dynamic_slice_in_dim(block, index * width, width, axis=1)


def to_slices(block, member):
    width = block.shape[1] // GROUP
    pieces = [feature_slice(block, member, width)]
    for mask in range(1, GROUP):
        pieces.append(flipped(feature_slice(block, member ^ mask, width), mask))
    return jnp.stack(pieces)


def to_rows(block, member):
    pieces = [block[0]] + [flipped(block[mask], mask) for mask in range(1, GROUP)]
    for bit in range(GROUP.bit_length() - 1):
        upper = (member >> bit & 1) == 1
        step = 1 << bit
        pieces = [jnp.where(upper, pieces[i ^ step], pieces[i]) for i in range(GROUP)]
    return jnp.concatenate(pieces, axis=1)


def over_groups(block):
    groups = block.shape[0]
    lists = [[g * GROUP + m for g in range(groups)] for m in range(GROUP)]
    return lax.all_to_all(
        block, "expert", split_axis=0, concat_axis=0, tiled=True, axis_index_groups=lists
    )


def shards(tokens, targets, routes, gate_ints, expert_home, gate_up, down_master, moment1, moment2):
    devices = lax.axis_size("expert")
    member = lax.axis_index("expert") % GROUP
    tok_rows, top_count = routes.shape
    feat_width = tokens.shape[1]
    width = feat_width // GROUP
    groups = devices // GROUP
    experts = expert_home.shape[0]
    capacity = (5 * tok_rows * top_count * GROUP + 4 * devices - 1) // (4 * devices)
    slot_rows = groups * capacity
    bf16, f32 = jnp.bfloat16, jnp.float32

    flat_ids = routes.reshape(-1)
    onehot = (flat_ids[:, None] == jnp.arange(experts, dtype=jnp.int32)[None, :]).astype(jnp.int32)
    slot_rank = jnp.sum((jnp.cumsum(onehot, axis=0) - onehot) * onehot, axis=1)
    slot_home = jnp.sum(onehot * expert_home[None, :], axis=1)
    slot_dest = (slot_home * capacity + slot_rank).reshape(tok_rows, top_count)

    row_ids = jnp.arange(slot_rows, dtype=jnp.int32)
    pick_own = jnp.zeros((slot_rows, tok_rows), jnp.bool_)
    for k in range(top_count):
        pick_own = pick_own | (row_ids[:, None] == slot_dest[:, k][None, :])
    outgoing = jnp.dot(
        pick_own.astype(bf16), tokens, preferred_element_type=f32
    ).astype(bf16).reshape(groups, capacity, feat_width)

    plan = member_gather(
        jnp.stack([slot_dest.T, gate_ints.T], axis=1)[None], 0
    )
    all_dest, all_gates = plan[:, :, 0], plan[:, :, 1]
    weights = all_gates.astype(f32) / 4096.0
    picks = (all_dest[:, :, :, None] == row_ids).astype(bf16)

    arrived = member_gather(over_groups(outgoing), 1)
    rows = groups * GROUP * capacity
    arrived = arrived.reshape(rows, feat_width)

    master = to_slices(down_master.astype(bf16), member)
    goal = to_slices(targets, member)
    moment_one = to_slices(moment1.astype(bf16), member)
    moment_two = to_slices(moment2.astype(bf16), member)
    units = master.shape[1]
    flat = (GROUP * units, width)
    master = master.reshape(flat).astype(f32)
    moment_one = moment_one.reshape(flat).astype(f32)
    moment_two = moment_two.reshape(flat).astype(f32)
    goal = goal.astype(f32)

    gate_acts = lax.dot_general(
        arrived, gate_up[0], (((1,), (1,)), ((), ())), preferred_element_type=f32
    )
    up_acts = lax.dot_general(
        arrived, gate_up[1], (((1,), (1,)), ((), ())), preferred_element_type=f32
    )
    own_hidden = (jax.nn.silu(gate_acts) * up_acts).astype(bf16)
    across = flipped(own_hidden, 2)
    hiddens = [own_hidden, flipped(own_hidden, 1), across, flipped(across, 1)]
    hidden = jnp.concatenate(
        [
            jnp.stack(
                [block.reshape(groups, GROUP, capacity, -1)[:, i ^ mask] for i in range(GROUP)],
                axis=1,
            ).reshape(rows, -1)
            for mask, block in enumerate(hiddens)
        ],
        axis=1,
    )

    moved = jnp.zeros(flat, f32)
    for round_index in range(2):
        summed = jnp.dot(hidden, master.astype(bf16), preferred_element_type=f32).astype(bf16)
        returned = over_groups(summed.reshape(groups, GROUP, capacity, width))
        returned = returned.transpose(1, 0, 2, 3).reshape(GROUP, slot_rows, width)
        mixed = jnp.zeros((GROUP, tok_rows, width), f32)
        for k in range(top_count):
            picked = jnp.einsum(
                "mts,msc->mtc", picks[:, k], returned, preferred_element_type=f32
            )
            mixed = mixed + weights[:, k, :, None] * picked
        residual = (mixed - goal) * loss_scale
        slot_values = (weights[:, :, :, None] * residual[:, None]).astype(bf16)
        grads_out = jnp.einsum(
            "mks,mkc->msc",
            picks.reshape(GROUP, top_count * tok_rows, slot_rows),
            slot_values.reshape(GROUP, top_count * tok_rows, width),
            preferred_element_type=f32,
        ).astype(bf16)
        grads_out = grads_out.reshape(GROUP, groups, capacity, width).transpose(1, 0, 2, 3)
        grad_rows = over_groups(grads_out).reshape(rows, width)
        gradient = lax.dot_general(
            hidden, grad_rows, (((0,), (0,)), ((), ())), preferred_element_type=f32
        )
        count = round_index + 1
        moment_one = 0.9 * moment_one + 0.1 * gradient
        moment_two = 0.999 * moment_two + 0.001 * gradient * gradient
        first_fix = 1.0 - 0.9 ** (prior_steps + count)
        second_fix = 1.0 - 0.999 ** (prior_steps + count)
        change = (moment_one / first_fix) / (jnp.sqrt(moment_two / second_fix) + epsilon)
        moved = moved + change
        master = master - learn_rate * change
    shape = (GROUP, units, width)
    return (
        to_rows(moved.astype(bf16).reshape(shape), member).astype(f32),
        to_rows(moment_one.astype(bf16).reshape(shape), member).astype(f32),
    )


def solution(mesh):
    in_specs = (
        P("expert", None),
        P("expert", None),
        P(("cand", "expert"), None),
        P(("cand", "expert"), None),
        P("cand"),
        P(None, ("cand", "expert"), None),
        P(("cand", "expert"), None),
        P(("cand", "expert"), None),
        P(("cand", "expert"), None),
    )
    out_specs = (P(("cand", "expert"), None), P(("cand", "expert"), None))
    return jax.shard_map(shards, mesh=mesh, in_specs=in_specs, out_specs=out_specs, check_vma=False)
```

```python
import functools

import jax
import jax.numpy as jnp
from jax import lax
from jax.experimental import pallas as pl
from jax.experimental.pallas import tpu as pltpu
from jax.sharding import PartitionSpec as P

GROUP = 4


learn_rate = 0.02
epsilon = 1e-08
prior_steps = 20
loss_scale = 0.125


def flipped(block, mask):
    count = lax.axis_size("expert")
    return lax.ppermute(block, "expert", [(i, i ^ mask) for i in range(count)])


def member_gather(block, axis):
    across = flipped(block, 2)
    near = flipped(block, 1)
    far = flipped(across, 1)
    return jnp.concatenate([block, near, across, far], axis=axis)


def feature_slice(block, index, width):
    return lax.dynamic_slice_in_dim(block, index * width, width, axis=1)


def to_slices(block, member):
    width = block.shape[1] // GROUP
    pieces = [feature_slice(block, member, width)]
    for mask in range(1, GROUP):
        pieces.append(flipped(feature_slice(block, member ^ mask, width), mask))
    return jnp.stack(pieces)


def to_rows(block, member):
    pieces = [block[0]] + [flipped(block[mask], mask) for mask in range(1, GROUP)]
    for bit in range(GROUP.bit_length() - 1):
        upper = (member >> bit & 1) == 1
        step = 1 << bit
        pieces = [jnp.where(upper, pieces[i ^ step], pieces[i]) for i in range(GROUP)]
    return jnp.concatenate(pieces, axis=1)


def over_groups(block):
    groups = block.shape[0]
    lists = [[g * GROUP + m for g in range(groups)] for m in range(GROUP)]
    return lax.all_to_all(
        block, "expert", split_axis=0, concat_axis=0, tiled=True, axis_index_groups=lists
    )


CHUNKS = 2


def rounds_kernel(
    groups, block, hidden, hidden_t, picks, picks_t, weights, goal, master, first, second,
    moved_out, first_out,
    sum_out, sum_in, grad_out, grad_in, values, master_two, first_two, second_two, moved_one,
    send_sems, recv_sems,
):
    bf16, f32 = jnp.bfloat16, jnp.float32
    here = lax.axis_index("expert")
    me, member = here // GROUP, lax.rem(here, GROUP)
    units, width = master.shape
    tokens = goal.shape[0]
    top_count = picks.shape[0]
    part = width // CHUNKS
    unit_tile = units // GROUP
    tok_tile = tokens // GROUP

    barrier = pltpu.get_barrier_semaphore()
    for d in range(1, groups):
        peer = lax.rem(me + d, groups) * GROUP + member
        pl.semaphore_signal(
            barrier, inc=1, device_id={"expert": peer}, device_id_type=pl.DeviceIdType.MESH
        )
    pl.semaphore_wait(barrier, groups - 1)

    def rows_of(group):
        return pl.ds(pl.multiple_of(group * block, block), block)

    def copy_to(source, target, phase, chunk, d):
        ahead = lax.rem(me + d, groups)
        return pltpu.make_async_remote_copy(
            src_ref=source.at[phase // 2, chunk, rows_of(ahead)],
            dst_ref=target.at[phase // 2, chunk, rows_of(me)],
            send_sem=send_sems.at[phase, chunk, d - 1],
            recv_sem=recv_sems.at[phase, chunk, d - 1],
            device_id={"expert": ahead * GROUP + member},
            device_id_type=pl.DeviceIdType.MESH,
        )

    order = list(range(1, groups)) + [0]

    def spread(left, right, source, target, phase, chunk):
        for d in order:
            ahead = lax.rem(me + d, groups)
            result = jnp.dot(
                left[rows_of(ahead)], right, preferred_element_type=f32
            ).astype(bf16)
            if d:
                source[phase // 2, chunk, rows_of(ahead)] = result
                copy_to(source, target, phase, chunk, d).start()
            else:
                target[phase // 2, chunk, rows_of(ahead)] = result

    def arrive(source, target, phase, chunk):
        for d in range(1, groups):
            copy_to(source, target, phase, chunk, d).wait_recv()

    def columns(chunk):
        return pl.ds(chunk * part, part)

    def forward(step, chunk):
        weight = master if step == 0 else master_two
        spread(hidden, weight[:, columns(chunk)], sum_out, sum_in, 2 * step, chunk)

    def residuals(step, chunk):
        arrive(sum_out, sum_in, 2 * step, chunk)

        @pl.loop(0, GROUP)
        def _(tile):
            span = pl.ds(pl.multiple_of(tile * tok_tile, tok_tile), tok_tile)
            mixed = jnp.zeros((tok_tile, part), f32)
            for k in range(top_count):
                mixed = mixed + weights[k, span] * jnp.dot(
                    picks[k, span], sum_in[step, chunk], preferred_element_type=f32
                )
            residual = (mixed - goal[span, columns(chunk)].astype(f32)) * loss_scale
            for k in range(top_count):
                place = pl.ds(
                    pl.multiple_of(k * tokens + tile * tok_tile, tok_tile), tok_tile
                )
                values[place] = (weights[k, span] * residual).astype(bf16)

        spread(picks_t, values[...], grad_out, grad_in, 2 * step + 1, chunk)

    def update(step, chunk):
        arrive(grad_out, grad_in, 2 * step + 1, chunk)
        count = step + 1
        first_fix = 1.0 - 0.9 ** (prior_steps + count)
        second_fix = 1.0 - 0.999 ** (prior_steps + count)
        cols = columns(chunk)

        @pl.loop(0, GROUP)
        def _(tile):
            span = pl.ds(pl.multiple_of(tile * unit_tile, unit_tile), unit_tile)
            gradient = jnp.dot(
                hidden_t[span], grad_in[step, chunk], preferred_element_type=f32
            )
            one = (first if step == 0 else first_two)[span, cols].astype(f32)
            two = (second if step == 0 else second_two)[span, cols].astype(f32)
            one = 0.9 * one + 0.1 * gradient
            two = 0.999 * two + 0.001 * gradient * gradient
            change = (one / first_fix) / (jnp.sqrt(two / second_fix) + epsilon)
            if step == 0:
                first_two[span, cols] = one
                second_two[span, cols] = two
                moved_one[span, cols] = change
                old = master[span, cols].astype(f32)
                master_two[span, cols] = (old - learn_rate * change).astype(bf16)
            else:
                moved_out[span, cols] = (moved_one[span, cols] + change).astype(bf16)
                first_out[span, cols] = one.astype(bf16)

    for chunk in range(CHUNKS):
        forward(0, chunk)
    for step in range(2):
        for chunk in range(CHUNKS):
            residuals(step, chunk)
        for chunk in range(CHUNKS):
            update(step, chunk)
            if step == 0:
                forward(1, chunk)
    for phase in range(4):
        source, target = ((sum_out, sum_in), (grad_out, grad_in))[phase % 2]
        for chunk in range(CHUNKS):
            for d in range(1, groups):
                copy_to(source, target, phase, chunk, d).wait_send()


def refit(groups, block, hidden, hidden_t, picks, picks_t, weights, goal, master, first, second):
    bf16, f32 = jnp.bfloat16, jnp.float32
    units, width = master.shape
    rows = hidden.shape[0]
    travel = pltpu.VMEM((2, CHUNKS, rows, width // CHUNKS), bf16)
    state = pltpu.VMEM((units, width), f32)
    sems = pltpu.SemaphoreType.DMA((4, CHUNKS, groups - 1))
    spec = pl.BlockSpec(memory_space=pltpu.VMEM)
    return pl.pallas_call(
        functools.partial(rounds_kernel, groups, block),
        out_shape=[jax.ShapeDtypeStruct((units, width), bf16)] * 2,
        in_specs=[spec] * 9,
        out_specs=[spec] * 2,
        scratch_shapes=[
            travel, travel, travel, travel,
            pltpu.VMEM((picks_t.shape[1], width // CHUNKS), bf16),
            pltpu.VMEM((units, width), bf16),
            state, state, state,
            sems, sems,
        ],
        compiler_params=pltpu.CompilerParams(
            collective_id=0, has_side_effects=True, vmem_limit_bytes=60 * 2**20
        ),
    )(hidden, hidden_t, picks, picks_t, weights, goal, master, first, second)


def shards(tokens, targets, routes, gate_ints, expert_home, gate_up, down_master, moment1, moment2):
    devices = lax.axis_size("expert")
    member = lax.axis_index("expert") % GROUP
    tok_rows, top_count = routes.shape
    feat_width = tokens.shape[1]
    width = feat_width // GROUP
    groups = devices // GROUP
    experts = expert_home.shape[0]
    capacity = (5 * tok_rows * top_count * GROUP + 4 * devices - 1) // (4 * devices)
    slot_rows = groups * capacity
    bf16, f32 = jnp.bfloat16, jnp.float32

    flat_ids = routes.reshape(-1)
    onehot = (flat_ids[:, None] == jnp.arange(experts, dtype=jnp.int32)[None, :]).astype(jnp.int32)
    slot_rank = jnp.sum((jnp.cumsum(onehot, axis=0) - onehot) * onehot, axis=1)
    slot_home = jnp.sum(onehot * expert_home[None, :], axis=1)
    slot_dest = (slot_home * capacity + slot_rank).reshape(tok_rows, top_count)

    row_ids = jnp.arange(slot_rows, dtype=jnp.int32)
    pick_own = jnp.zeros((slot_rows, tok_rows), jnp.bool_)
    for k in range(top_count):
        pick_own = pick_own | (row_ids[:, None] == slot_dest[:, k][None, :])
    outgoing = jnp.dot(
        pick_own.astype(bf16), tokens, preferred_element_type=f32
    ).astype(bf16).reshape(groups, capacity, feat_width)

    plan = member_gather(
        jnp.stack([slot_dest.T, gate_ints.T], axis=1)[None], 0
    )
    all_dest, all_gates = plan[:, :, 0], plan[:, :, 1]
    block = -(-GROUP * capacity // 16) * 16
    rows = groups * block
    offsets = (jnp.arange(GROUP, dtype=jnp.int32) * capacity)[:, None, None]
    all_dest = all_dest // capacity * block + all_dest % capacity + offsets
    by_choice = all_dest.transpose(1, 0, 2).reshape(top_count, GROUP * tok_rows)
    weights = all_gates.transpose(1, 0, 2).reshape(top_count, GROUP * tok_rows, 1)
    weights = weights.astype(f32) / 4096.0
    buffer_ids = jnp.arange(rows, dtype=jnp.int32)
    picks = (by_choice[:, :, None] == buffer_ids).astype(bf16)
    picks_t = (buffer_ids[:, None] == by_choice.reshape(-1)).astype(bf16)

    arrived = member_gather(over_groups(outgoing), 1)
    arrived = jnp.pad(arrived, ((0, 0), (0, block - GROUP * capacity), (0, 0)))
    arrived = arrived.reshape(rows, feat_width)

    master = to_slices(down_master.astype(bf16), member)
    goal = to_slices(targets, member)
    moment_one = to_slices(moment1.astype(bf16), member)
    moment_two = to_slices(moment2.astype(bf16), member)
    units = master.shape[1]
    flat = (GROUP * units, width)
    master = master.reshape(flat)
    moment_one = moment_one.reshape(flat)
    moment_two = moment_two.reshape(flat)
    goal = goal.reshape(GROUP * tok_rows, width)

    gate_acts = lax.dot_general(
        arrived, gate_up[0], (((1,), (1,)), ((), ())), preferred_element_type=f32
    )
    up_acts = lax.dot_general(
        arrived, gate_up[1], (((1,), (1,)), ((), ())), preferred_element_type=f32
    )
    def reordered(piece, mask):
        piece = piece.reshape(groups, block, -1)
        parts = [
            piece[:, (i ^ mask) * capacity : ((i ^ mask) + 1) * capacity] for i in range(GROUP)
        ]
        parts.append(piece[:, GROUP * capacity :])
        return jnp.concatenate(parts, axis=1).reshape(rows, -1)

    own_hidden = (jax.nn.silu(gate_acts) * up_acts).astype(bf16)
    across = flipped(own_hidden, 2)
    hiddens = [own_hidden, flipped(own_hidden, 1), across, flipped(across, 1)]
    hidden = jnp.concatenate(
        [
            reordered(piece, mask)
            for mask, piece in enumerate(hiddens)
        ],
        axis=1,
    )

    moved, moment_one = refit(
        groups, block, hidden, hidden.T, picks, picks_t, weights, goal,
        master, moment_one, moment_two,
    )
    shape = (GROUP, units, width)
    return (
        to_rows(moved.reshape(shape), member).astype(f32),
        to_rows(moment_one.reshape(shape), member).astype(f32),
    )


def solution(mesh):
    in_specs = (
        P("expert", None),
        P("expert", None),
        P(("cand", "expert"), None),
        P(("cand", "expert"), None),
        P("cand"),
        P(None, ("cand", "expert"), None),
        P(("cand", "expert"), None),
        P(("cand", "expert"), None),
        P(("cand", "expert"), None),
    )
    out_specs = (P(("cand", "expert"), None), P(("cand", "expert"), None))
    return jax.shard_map(shards, mesh=mesh, in_specs=in_specs, out_specs=out_specs, check_vma=False)
```

```python
import functools

import jax
import jax.numpy as jnp
from jax import lax
from jax.experimental import pallas as pl
from jax.experimental.pallas import tpu as pltpu
from jax.sharding import PartitionSpec as P

GROUP = 4


learn_rate = 0.02
epsilon = 1e-08
prior_steps = 20
loss_scale = 0.125


def flipped(block, mask):
    count = lax.axis_size("expert")
    return lax.ppermute(block, "expert", [(i, i ^ mask) for i in range(count)])


def partner_of(member, mask):
    low, high = lax.rem(member, 2), member // 2
    return member + (mask & 1) * (1 - 2 * low) + (mask & 2) * (1 - 2 * high)


def greet(peers):
    barrier = pltpu.get_barrier_semaphore()
    for peer in peers:
        pl.semaphore_signal(
            barrier, inc=1, device_id={"expert": peer}, device_id_type=pl.DeviceIdType.MESH
        )
    pl.semaphore_wait(barrier, len(peers))


def push(source, target, send_sem, recv_sem, peer):
    return pltpu.make_async_remote_copy(
        src_ref=source,
        dst_ref=target,
        send_sem=send_sem,
        recv_sem=recv_sem,
        device_id={"expert": peer},
        device_id_type=pl.DeviceIdType.MESH,
    )


def slice_copy(source, target, sends, recvs, base, member, mask, start, count):
    rows, width = source.shape[0], target.shape[1]
    partner = partner_of(member, mask)
    return push(
        source.at[:, pl.ds(pl.multiple_of(partner * width + start, 128), count)],
        target.at[pl.ds(mask * rows, rows), pl.ds(start, count)],
        sends, recvs, base + partner,
    )


def dispatch_kernel(
    groups, capacity, outgoing, gate_up, master, targets,
    hidden, master_in, goal_in,
    arrived, group_send, group_recv, row_send, row_recv, unit_send, unit_recv,
    state_send, state_recv,
):
    bf16, f32 = jnp.bfloat16, jnp.float32
    here = lax.axis_index("expert")
    me, member = here // GROUP, lax.rem(here, GROUP)
    base = me * GROUP
    units = gate_up.shape[1]
    block = GROUP * capacity
    greet(
        [lax.rem(me + d, groups) * GROUP + member for d in range(1, groups)]
        + [base + partner_of(member, mask) for mask in range(1, GROUP)]
    )

    def rows_of(group, part):
        return pl.ds(pl.multiple_of(group * block + part * capacity, capacity), capacity)

    def group_copy(d):
        ahead = lax.rem(me + d, groups)
        return push(
            outgoing.at[pl.ds(pl.multiple_of(ahead * capacity, capacity), capacity)],
            arrived.at[rows_of(me, 0)],
            group_send.at[d - 1], group_recv.at[d - 1], ahead * GROUP + member,
        )

    def source_of(d):
        return lax.rem(me + groups - d, groups)

    def row_copy(d, mask):
        group = source_of(d)
        if mask == 3:
            source, peer = arrived.at[rows_of(group, 2)], partner_of(member, 1)
        elif d == 0:
            source = outgoing.at[pl.ds(pl.multiple_of(me * capacity, capacity), capacity)]
            peer = partner_of(member, mask)
        else:
            source, peer = arrived.at[rows_of(group, 0)], partner_of(member, mask)
        return push(
            source, arrived.at[rows_of(group, mask)],
            row_send.at[d, mask - 1], row_recv.at[d, mask - 1], base + peer,
        )

    def unit_copy(d, mask, part):
        group = source_of(d)
        flip = 1 if mask == 3 else mask
        origin = 2 if mask == 3 else 0
        return push(
            hidden.at[rows_of(group, part), pl.ds(origin * units, units)],
            hidden.at[rows_of(group, part ^ flip), pl.ds(mask * units, units)],
            unit_send.at[d, mask - 1, part], unit_recv.at[d, mask - 1, part],
            base + partner_of(member, flip),
        )

    states = ((master, master_in), (targets, goal_in))

    def state_copy(which, mask):
        source, target = states[which]
        return slice_copy(
            source, target, state_send.at[which, mask - 1], state_recv.at[which, mask - 1],
            base, member, mask, 0, target.shape[1],
        )

    order = sorted(range(1, groups), key=lambda d: min(d, groups - d))
    for d in reversed(order):
        group_copy(d).start()
    row_copy(0, 2).start()
    row_copy(0, 1).start()
    for mask in (2, 3, 1):
        state_copy(0, mask).start()
    mine = pl.ds(pl.multiple_of(me * capacity, capacity), capacity)
    arrived[rows_of(me, 0)] = outgoing[mine]
    for source, target in states:
        rows, width = source.shape[0], target.shape[1]
        target[pl.ds(0, rows)] = source[:, pl.ds(pl.multiple_of(member * width, 128), width)]

    def relay(d):
        row_copy(d, 2).wait_recv()
        row_copy(d, 3).start()

    def compute(d):
        row_copy(d, 1).wait_recv()
        row_copy(d, 3).wait_recv()
        span = pl.ds(pl.multiple_of(source_of(d) * block, block), block)
        acts = [
            lax.dot_general(
                arrived[span], gate_up[i], (((1,), (1,)), ((), ())), preferred_element_type=f32
            )
            for i in range(2)
        ]
        gated = acts[0] / (1.0 + jnp.exp(-acts[0])) * acts[1]
        hidden[span, pl.ds(0, units)] = gated.astype(bf16)
        for mask in (2, 1):
            for part in range(GROUP):
                unit_copy(d, mask, part).start()

    chain = [0] + order
    for d in order:
        group_copy(d).wait_recv()
        row_copy(d, 2).start()
        row_copy(d, 1).start()
    for mask in (2, 3, 1):
        state_copy(1, mask).start()
    for position, d in enumerate(chain):
        relay(d)
        if position:
            compute(chain[position - 1])
    compute(chain[-1])
    for d in chain:
        for part in range(GROUP):
            unit_copy(d, 2, part).wait_recv()
        for part in range(GROUP):
            unit_copy(d, 3, part).start()
    for d in chain:
        for part in range(GROUP):
            unit_copy(d, 1, part).wait_recv()
            unit_copy(d, 3, part).wait_recv()
    for which in range(2):
        for mask in range(1, GROUP):
            state_copy(which, mask).wait()
    for d in order:
        group_copy(d).wait_send()
    for d in chain:
        for mask in range(1, GROUP):
            row_copy(d, mask).wait_send()
            for part in range(GROUP):
                unit_copy(d, mask, part).wait_send()


def dispatch(groups, capacity, outgoing, gate_up, master, targets):
    bf16 = jnp.bfloat16
    units, feat_width = master.shape
    width = feat_width // GROUP
    rows = groups * GROUP * capacity
    spec = pl.BlockSpec(memory_space=pltpu.VMEM)
    pair = lambda *shape: [pltpu.SemaphoreType.DMA(shape)] * 2
    return pl.pallas_call(
        functools.partial(dispatch_kernel, groups, capacity),
        out_shape=[
            jax.ShapeDtypeStruct((rows, GROUP * units), bf16),
            jax.ShapeDtypeStruct((GROUP * units, width), bf16),
            jax.ShapeDtypeStruct((GROUP * targets.shape[0], width), bf16),
        ],
        in_specs=[spec] * 4,
        out_specs=[spec] * 3,
        scratch_shapes=[
            pltpu.VMEM((rows, feat_width), bf16),
            *pair(groups - 1), *pair(groups, 3), *pair(groups, 3, GROUP), *pair(2, 3),
        ],
        compiler_params=pltpu.CompilerParams(
            collective_id=1, has_side_effects=True, vmem_limit_bytes=60 * 2**20
        ),
    )(outgoing, gate_up, master, targets)


def member_gather(block, axis):
    across = flipped(block, 2)
    near = flipped(block, 1)
    far = flipped(across, 1)
    return jnp.concatenate([block, near, across, far], axis=axis)


def to_rows(block, member):
    pieces = [block[0]] + [flipped(block[mask], mask) for mask in range(1, GROUP)]
    for bit in range(GROUP.bit_length() - 1):
        upper = (member >> bit & 1) == 1
        step = 1 << bit
        pieces = [jnp.where(upper, pieces[i ^ step], pieces[i]) for i in range(GROUP)]
    return jnp.concatenate(pieces, axis=1)


CHUNKS = 2


def rounds_kernel(
    groups, block, hidden, hidden_t, picks, picks_t, weights, goal, master, first, second,
    moved_out, first_out,
    sum_out, sum_in, grad_out, grad_in, values, master_two, first_two, second_two, moved_one,
    first_in, second_in, send_sems, recv_sems, state_send, state_recv,
):
    bf16, f32 = jnp.bfloat16, jnp.float32
    here = lax.axis_index("expert")
    me, member = here // GROUP, lax.rem(here, GROUP)
    units, width = master.shape
    tokens = goal.shape[0]
    top_count = picks.shape[0]
    part = width // CHUNKS
    unit_tile = units // GROUP
    tok_tile = tokens // GROUP

    base = me * GROUP
    greet(
        [lax.rem(me + d, groups) * GROUP + member for d in range(1, groups)]
        + [base + partner_of(member, mask) for mask in range(1, GROUP)]
    )
    states = ((first, first_in), (second, second_in))

    def state_copy(which, chunk, mask):
        source, target = states[which]
        return slice_copy(
            source, target, state_send.at[which, chunk, mask - 1],
            state_recv.at[which, chunk, mask - 1], base, member, mask, chunk * part, part,
        )

    def rows_of(group):
        return pl.ds(pl.multiple_of(group * block, block), block)

    def copy_to(source, target, phase, chunk, d):
        ahead = lax.rem(me + d, groups)
        return pltpu.make_async_remote_copy(
            src_ref=source.at[phase // 2, chunk, rows_of(ahead)],
            dst_ref=target.at[phase // 2, chunk, rows_of(me)],
            send_sem=send_sems.at[phase, chunk, d - 1],
            recv_sem=recv_sems.at[phase, chunk, d - 1],
            device_id={"expert": ahead * GROUP + member},
            device_id_type=pl.DeviceIdType.MESH,
        )

    order = list(range(1, groups)) + [0]

    def spread(left, right, source, target, phase, chunk):
        for d in order:
            ahead = lax.rem(me + d, groups)
            result = jnp.dot(
                left[rows_of(ahead)], right, preferred_element_type=f32
            ).astype(bf16)
            if d:
                source[phase // 2, chunk, rows_of(ahead)] = result
                copy_to(source, target, phase, chunk, d).start()
            else:
                target[phase // 2, chunk, rows_of(ahead)] = result

    def arrive(source, target, phase, chunk):
        for d in range(1, groups):
            copy_to(source, target, phase, chunk, d).wait_recv()

    def columns(chunk):
        return pl.ds(chunk * part, part)

    def forward(step, chunk):
        weight = master if step == 0 else master_two
        spread(hidden, weight[:, columns(chunk)], sum_out, sum_in, 2 * step, chunk)

    def residuals(step, chunk):
        arrive(sum_out, sum_in, 2 * step, chunk)

        @pl.loop(0, GROUP)
        def _(tile):
            span = pl.ds(pl.multiple_of(tile * tok_tile, tok_tile), tok_tile)
            mixed = jnp.zeros((tok_tile, part), f32)
            for k in range(top_count):
                mixed = mixed + weights[k, span] * jnp.dot(
                    picks[k, span], sum_in[step, chunk], preferred_element_type=f32
                )
            residual = (mixed - goal[span, columns(chunk)].astype(f32)) * loss_scale
            for k in range(top_count):
                place = pl.ds(
                    pl.multiple_of(k * tokens + tile * tok_tile, tok_tile), tok_tile
                )
                values[place] = (weights[k, span] * residual).astype(bf16)

        spread(picks_t, values[...], grad_out, grad_in, 2 * step + 1, chunk)

    def update(step, chunk):
        arrive(grad_out, grad_in, 2 * step + 1, chunk)
        if step == 0:
            for which in range(2):
                for mask in range(1, GROUP):
                    state_copy(which, chunk, mask).wait()
        count = step + 1
        first_fix = 1.0 - 0.9 ** (prior_steps + count)
        second_fix = 1.0 - 0.999 ** (prior_steps + count)
        cols = columns(chunk)

        @pl.loop(0, GROUP)
        def _(tile):
            span = pl.ds(pl.multiple_of(tile * unit_tile, unit_tile), unit_tile)
            gradient = jnp.dot(
                hidden_t[span], grad_in[step, chunk], preferred_element_type=f32
            )
            one = (first_in if step == 0 else first_two)[span, cols]
            two = (second_in if step == 0 else second_two)[span, cols]
            one = 0.9 * one + 0.1 * gradient
            two = 0.999 * two + 0.001 * gradient * gradient
            change = (one / first_fix) / (jnp.sqrt(two / second_fix) + epsilon)
            if step == 0:
                first_two[span, cols] = one
                second_two[span, cols] = two
                moved_one[span, cols] = change
                old = master[span, cols].astype(f32)
                master_two[span, cols] = (old - learn_rate * change).astype(bf16)
            else:
                moved_out[span, cols] = (moved_one[span, cols] + change).astype(bf16)
                first_out[span, cols] = one.astype(bf16)

    for chunk in range(CHUNKS):
        for which in range(2):
            for mask in (2, 3, 1):
                state_copy(which, chunk, mask).start()
    for chunk in range(CHUNKS):
        forward(0, chunk)
    for source, target in states:
        target[pl.ds(0, source.shape[0])] = source[
            :, pl.ds(pl.multiple_of(member * width, 128), width)
        ]
    for step in range(2):
        for chunk in range(CHUNKS):
            residuals(step, chunk)
        for chunk in range(CHUNKS):
            update(step, chunk)
            if step == 0:
                forward(1, chunk)
    for phase in range(4):
        source, target = ((sum_out, sum_in), (grad_out, grad_in))[phase % 2]
        for chunk in range(CHUNKS):
            for d in range(1, groups):
                copy_to(source, target, phase, chunk, d).wait_send()


def refit(groups, block, hidden, hidden_t, picks, picks_t, weights, goal, master, first, second):
    bf16, f32 = jnp.bfloat16, jnp.float32
    units, width = master.shape
    rows = hidden.shape[0]
    travel = pltpu.VMEM((2, CHUNKS, rows, width // CHUNKS), bf16)
    state = pltpu.VMEM((units, width), f32)
    sems = pltpu.SemaphoreType.DMA((4, CHUNKS, groups - 1))
    spec = pl.BlockSpec(memory_space=pltpu.VMEM)
    return pl.pallas_call(
        functools.partial(rounds_kernel, groups, block),
        out_shape=[jax.ShapeDtypeStruct((units, width), bf16)] * 2,
        in_specs=[spec] * 9,
        out_specs=[spec] * 2,
        scratch_shapes=[
            travel, travel, travel, travel,
            pltpu.VMEM((picks_t.shape[1], width // CHUNKS), bf16),
            pltpu.VMEM((units, width), bf16),
            state, state, state, state, state,
            sems, sems,
            pltpu.SemaphoreType.DMA((2, CHUNKS, 3)), pltpu.SemaphoreType.DMA((2, CHUNKS, 3)),
        ],
        compiler_params=pltpu.CompilerParams(
            collective_id=0, has_side_effects=True, vmem_limit_bytes=60 * 2**20
        ),
    )(hidden, hidden_t, picks, picks_t, weights, goal, master, first, second)


def shards(tokens, targets, routes, gate_ints, expert_home, gate_up, down_master, moment1, moment2):
    devices = lax.axis_size("expert")
    member = lax.axis_index("expert") % GROUP
    tok_rows, top_count = routes.shape
    feat_width = tokens.shape[1]
    width = feat_width // GROUP
    groups = devices // GROUP
    experts = expert_home.shape[0]
    capacity = (5 * tok_rows * top_count * GROUP + 4 * devices - 1) // (4 * devices)
    capacity = -(-capacity // 16) * 16
    slot_rows = groups * capacity
    bf16, f32 = jnp.bfloat16, jnp.float32

    flat_ids = routes.reshape(-1)
    onehot = (flat_ids[:, None] == jnp.arange(experts, dtype=jnp.int32)[None, :]).astype(jnp.int32)
    slot_rank = jnp.sum((jnp.cumsum(onehot, axis=0) - onehot) * onehot, axis=1)
    slot_home = jnp.sum(onehot * expert_home[None, :], axis=1)
    slot_dest = (slot_home * capacity + slot_rank).reshape(tok_rows, top_count)

    row_ids = jnp.arange(slot_rows, dtype=jnp.int32)
    pick_own = jnp.zeros((slot_rows, tok_rows), jnp.bool_)
    for k in range(top_count):
        pick_own = pick_own | (row_ids[:, None] == slot_dest[:, k][None, :])
    outgoing = jnp.dot(
        pick_own.astype(bf16), tokens, preferred_element_type=f32
    ).astype(bf16)

    plan = member_gather(
        jnp.stack([slot_dest.T, gate_ints.T], axis=1)[None], 0
    )
    all_dest, all_gates = plan[:, :, 0], plan[:, :, 1]
    block = GROUP * capacity
    rows = groups * block
    offsets = (jnp.arange(GROUP, dtype=jnp.int32) * capacity)[:, None, None]
    all_dest = all_dest // capacity * block + all_dest % capacity + offsets
    by_choice = all_dest.transpose(1, 0, 2).reshape(top_count, GROUP * tok_rows)
    weights = all_gates.transpose(1, 0, 2).reshape(top_count, GROUP * tok_rows, 1)
    weights = weights.astype(f32) / 4096.0
    buffer_ids = jnp.arange(rows, dtype=jnp.int32)
    picks = (by_choice[:, :, None] == buffer_ids).astype(bf16)
    picks_t = (buffer_ids[:, None] == by_choice.reshape(-1)).astype(bf16)

    hidden, master, goal = dispatch(
        groups, capacity, outgoing, gate_up, down_master.astype(bf16), targets
    )
    units, width = down_master.shape[0], feat_width // GROUP
    moved, moment_one = refit(
        groups, block, hidden, hidden.T, picks, picks_t, weights, goal,
        master, moment1, moment2,
    )
    shape = (GROUP, units, width)
    return (
        to_rows(moved.reshape(shape), member).astype(f32),
        to_rows(moment_one.reshape(shape), member).astype(f32),
    )


def solution(mesh):
    in_specs = (
        P("expert", None),
        P("expert", None),
        P(("cand", "expert"), None),
        P(("cand", "expert"), None),
        P("cand"),
        P(None, ("cand", "expert"), None),
        P(("cand", "expert"), None),
        P(("cand", "expert"), None),
        P(("cand", "expert"), None),
    )
    out_specs = (P(("cand", "expert"), None), P(("cand", "expert"), None))
    return jax.shard_map(shards, mesh=mesh, in_specs=in_specs, out_specs=out_specs, check_vma=False)
```

```python
import functools

import jax
import jax.numpy as jnp
from jax import lax
from jax.experimental import pallas as pl
from jax.experimental.pallas import tpu as pltpu
from jax.sharding import PartitionSpec as P

GROUP = 4


learn_rate = 0.02
epsilon = 1e-08
prior_steps = 20
loss_scale = 0.125


def flipped(block, mask):
    count = lax.axis_size("expert")
    return lax.ppermute(block, "expert", [(i, i ^ mask) for i in range(count)])


def partner_of(member, mask):
    low, high = lax.rem(member, 2), member // 2
    return member + (mask & 1) * (1 - 2 * low) + (mask & 2) * (1 - 2 * high)


def greet(peers):
    barrier = pltpu.get_barrier_semaphore()
    for peer in peers:
        pl.semaphore_signal(
            barrier, inc=1, device_id={"expert": peer}, device_id_type=pl.DeviceIdType.MESH
        )
    pl.semaphore_wait(barrier, len(peers))


def push(source, target, send_sem, recv_sem, peer):
    return pltpu.make_async_remote_copy(
        src_ref=source,
        dst_ref=target,
        send_sem=send_sem,
        recv_sem=recv_sem,
        device_id={"expert": peer},
        device_id_type=pl.DeviceIdType.MESH,
    )


def slice_copy(source, target, sends, recvs, base, member, mask, start, count):
    rows, width = source.shape[0], target.shape[1]
    partner = partner_of(member, mask)
    return push(
        source.at[:, pl.ds(pl.multiple_of(partner * width + start, 128), count)],
        target.at[pl.ds(mask * rows, rows), pl.ds(start, count)],
        sends, recvs, base + partner,
    )


def dispatch_kernel(
    groups, capacity, outgoing, gate_up, master, targets,
    hidden, master_in, goal_in,
    arrived, group_send, group_recv, row_send, row_recv, unit_send, unit_recv,
    state_send, state_recv,
):
    bf16, f32 = jnp.bfloat16, jnp.float32
    here = lax.axis_index("expert")
    me, member = here // GROUP, lax.rem(here, GROUP)
    base = me * GROUP
    units = gate_up.shape[1]
    block = GROUP * capacity
    greet(
        [lax.rem(me + d, groups) * GROUP + member for d in range(1, groups)]
        + [base + partner_of(member, mask) for mask in range(1, GROUP)]
    )

    def rows_of(group, part):
        return pl.ds(pl.multiple_of(group * block + part * capacity, capacity), capacity)

    def group_copy(d):
        ahead = lax.rem(me + d, groups)
        return push(
            outgoing.at[pl.ds(pl.multiple_of(ahead * capacity, capacity), capacity)],
            arrived.at[rows_of(me, 0)],
            group_send.at[d - 1], group_recv.at[d - 1], ahead * GROUP + member,
        )

    def source_of(d):
        return lax.rem(me + groups - d, groups)

    def row_copy(d, mask):
        group = source_of(d)
        if mask == 3:
            source, peer = arrived.at[rows_of(group, 2)], partner_of(member, 1)
        elif d == 0:
            source = outgoing.at[pl.ds(pl.multiple_of(me * capacity, capacity), capacity)]
            peer = partner_of(member, mask)
        else:
            source, peer = arrived.at[rows_of(group, 0)], partner_of(member, mask)
        return push(
            source, arrived.at[rows_of(group, mask)],
            row_send.at[d, mask - 1], row_recv.at[d, mask - 1], base + peer,
        )

    def unit_copy(d, mask, part):
        group = source_of(d)
        flip = 1 if mask == 3 else mask
        origin = 2 if mask == 3 else 0
        return push(
            hidden.at[rows_of(group, part), pl.ds(origin * units, units)],
            hidden.at[rows_of(group, part ^ flip), pl.ds(mask * units, units)],
            unit_send.at[d, mask - 1, part], unit_recv.at[d, mask - 1, part],
            base + partner_of(member, flip),
        )

    states = ((master, master_in), (targets, goal_in))

    def state_copy(which, mask):
        source, target = states[which]
        return slice_copy(
            source, target, state_send.at[which, mask - 1], state_recv.at[which, mask - 1],
            base, member, mask, 0, target.shape[1],
        )

    order = sorted(range(1, groups), key=lambda d: min(d, groups - d))
    for d in reversed(order):
        group_copy(d).start()
    row_copy(0, 2).start()
    row_copy(0, 1).start()
    for mask in (2, 3, 1):
        state_copy(0, mask).start()
    mine = pl.ds(pl.multiple_of(me * capacity, capacity), capacity)
    arrived[rows_of(me, 0)] = outgoing[mine]
    for source, target in states:
        rows, width = source.shape[0], target.shape[1]
        target[pl.ds(0, rows)] = source[:, pl.ds(pl.multiple_of(member * width, 128), width)]

    def relay(d):
        row_copy(d, 2).wait_recv()
        row_copy(d, 3).start()

    def compute(d):
        row_copy(d, 1).wait_recv()
        row_copy(d, 3).wait_recv()
        span = pl.ds(pl.multiple_of(source_of(d) * block, block), block)
        acts = [
            lax.dot_general(
                arrived[span], gate_up[i], (((1,), (1,)), ((), ())), preferred_element_type=f32
            )
            for i in range(2)
        ]
        gated = acts[0] / (1.0 + jnp.exp(-acts[0])) * acts[1]
        hidden[span, pl.ds(0, units)] = gated.astype(bf16)
        for mask in (2, 1):
            for part in range(GROUP):
                unit_copy(d, mask, part).start()

    chain = [0] + order
    for d in order:
        group_copy(d).wait_recv()
        row_copy(d, 2).start()
        row_copy(d, 1).start()
    for mask in (2, 3, 1):
        state_copy(1, mask).start()
    for position, d in enumerate(chain):
        relay(d)
        if position:
            compute(chain[position - 1])
    compute(chain[-1])
    for d in chain:
        for part in range(GROUP):
            unit_copy(d, 2, part).wait_recv()
        for part in range(GROUP):
            unit_copy(d, 3, part).start()
    for d in chain:
        for part in range(GROUP):
            unit_copy(d, 1, part).wait_recv()
            unit_copy(d, 3, part).wait_recv()
    for which in range(2):
        for mask in range(1, GROUP):
            state_copy(which, mask).wait()
    for d in order:
        group_copy(d).wait_send()
    for d in chain:
        for mask in range(1, GROUP):
            row_copy(d, mask).wait_send()
            for part in range(GROUP):
                unit_copy(d, mask, part).wait_send()


def dispatch(groups, capacity, outgoing, gate_up, master, targets):
    bf16 = jnp.bfloat16
    units, feat_width = master.shape
    width = feat_width // GROUP
    rows = groups * GROUP * capacity
    spec = pl.BlockSpec(memory_space=pltpu.VMEM)
    pair = lambda *shape: [pltpu.SemaphoreType.DMA(shape)] * 2
    return pl.pallas_call(
        functools.partial(dispatch_kernel, groups, capacity),
        out_shape=[
            jax.ShapeDtypeStruct((rows, GROUP * units), bf16),
            jax.ShapeDtypeStruct((GROUP * units, width), bf16),
            jax.ShapeDtypeStruct((GROUP * targets.shape[0], width), bf16),
        ],
        in_specs=[spec] * 4,
        out_specs=[spec] * 3,
        scratch_shapes=[
            pltpu.VMEM((rows, feat_width), bf16),
            *pair(groups - 1), *pair(groups, 3), *pair(groups, 3, GROUP), *pair(2, 3),
        ],
        compiler_params=pltpu.CompilerParams(
            collective_id=1, has_side_effects=True, vmem_limit_bytes=60 * 2**20
        ),
    )(outgoing, gate_up, master, targets)


def member_gather(block, axis):
    across = flipped(block, 2)
    near = flipped(block, 1)
    far = flipped(across, 1)
    return jnp.concatenate([block, near, across, far], axis=axis)


CHUNKS = 2


def rounds_kernel(
    groups, block, hidden, dest, dest_t, weights, goal, master, first, second,
    moved_rows, first_rows,
    moved_out, first_out, picks, picks_t,
    sum_out, sum_in, grad_out, grad_in, values, master_two, first_two, second_two, moved_one,
    first_in, second_in, send_sems, recv_sems, state_send, state_recv, out_send, out_recv,
):
    bf16, f32 = jnp.bfloat16, jnp.float32
    here = lax.axis_index("expert")
    me, member = here // GROUP, lax.rem(here, GROUP)
    units, width = master.shape
    tokens = goal.shape[0]
    top_count = picks.shape[0]
    part = width // CHUNKS
    unit_tile = units // GROUP
    tok_tile = tokens // GROUP

    base = me * GROUP
    greet(
        [lax.rem(me + d, groups) * GROUP + member for d in range(1, groups)]
        + [base + partner_of(member, mask) for mask in range(1, GROUP)]
    )
    states = ((first, first_in), (second, second_in))

    def state_copy(which, chunk, mask):
        source, target = states[which]
        return slice_copy(
            source, target, state_send.at[which, chunk, mask - 1],
            state_recv.at[which, chunk, mask - 1], base, member, mask, chunk * part, part,
        )

    def rows_of(group):
        return pl.ds(pl.multiple_of(group * block, block), block)

    def copy_to(source, target, phase, chunk, d):
        ahead = lax.rem(me + d, groups)
        return pltpu.make_async_remote_copy(
            src_ref=source.at[phase // 2, chunk, rows_of(ahead)],
            dst_ref=target.at[phase // 2, chunk, rows_of(me)],
            send_sem=send_sems.at[phase, chunk, d - 1],
            recv_sem=recv_sems.at[phase, chunk, d - 1],
            device_id={"expert": ahead * GROUP + member},
            device_id_type=pl.DeviceIdType.MESH,
        )

    order = list(range(1, groups)) + [0]

    def spread(left, right, source, target, phase, chunk):
        for d in order:
            ahead = lax.rem(me + d, groups)
            result = jnp.dot(
                left[rows_of(ahead)], right, preferred_element_type=f32
            ).astype(bf16)
            if d:
                source[phase // 2, chunk, rows_of(ahead)] = result
                copy_to(source, target, phase, chunk, d).start()
            else:
                target[phase // 2, chunk, rows_of(ahead)] = result

    def arrive(source, target, phase, chunk):
        for d in range(1, groups):
            copy_to(source, target, phase, chunk, d).wait_recv()

    def columns(chunk):
        return pl.ds(chunk * part, part)

    def forward(step, chunk):
        weight = master if step == 0 else master_two
        spread(hidden, weight[:, columns(chunk)], sum_out, sum_in, 2 * step, chunk)

    def residuals(step, chunk):
        arrive(sum_out, sum_in, 2 * step, chunk)

        @pl.loop(0, GROUP)
        def _(tile):
            span = pl.ds(pl.multiple_of(tile * tok_tile, tok_tile), tok_tile)
            mixed = jnp.zeros((tok_tile, part), f32)
            for k in range(top_count):
                mixed = mixed + weights[k, span] * jnp.dot(
                    picks[k, span], sum_in[step, chunk], preferred_element_type=f32
                )
            residual = (mixed - goal[span, columns(chunk)].astype(f32)) * loss_scale
            for k in range(top_count):
                place = pl.ds(
                    pl.multiple_of(k * tokens + tile * tok_tile, tok_tile), tok_tile
                )
                values[place] = (weights[k, span] * residual).astype(bf16)

        spread(picks_t, values[...], grad_out, grad_in, 2 * step + 1, chunk)

    def update(step, chunk):
        arrive(grad_out, grad_in, 2 * step + 1, chunk)
        if step == 0:
            for which in range(2):
                for mask in range(1, GROUP):
                    state_copy(which, chunk, mask).wait()
        count = step + 1
        first_fix = 1.0 - 0.9 ** (prior_steps + count)
        second_fix = 1.0 - 0.999 ** (prior_steps + count)
        cols = columns(chunk)

        @pl.loop(0, GROUP)
        def _(tile):
            span = pl.ds(pl.multiple_of(tile * unit_tile, unit_tile), unit_tile)
            gradient = lax.dot_general(
                hidden[:, span], grad_in[step, chunk], (((0,), (0,)), ((), ())),
                preferred_element_type=f32,
            )
            one = (first_in if step == 0 else first_two)[span, cols]
            two = (second_in if step == 0 else second_two)[span, cols]
            one = 0.9 * one + 0.1 * gradient
            two = 0.999 * two + 0.001 * gradient * gradient
            change = (one / first_fix) / (jnp.sqrt(two / second_fix) + epsilon)
            if step == 0:
                first_two[span, cols] = one
                second_two[span, cols] = two
                moved_one[span, cols] = change
                old = master[span, cols].astype(f32)
                master_two[span, cols] = (old - learn_rate * change).astype(bf16)
            else:
                moved_out[span, cols] = (moved_one[span, cols] + change).astype(bf16)
                first_out[span, cols] = one.astype(bf16)

    results = ((moved_out, moved_rows), (first_out, first_rows))
    own_units = first.shape[0]

    def out_columns(chunk):
        return pl.ds(pl.multiple_of(member * width + chunk * part, 128), part)

    def out_copy(which, chunk, mask):
        source, target = results[which]
        return push(
            source.at[pl.ds(mask * own_units, own_units), columns(chunk)],
            target.at[:, out_columns(chunk)],
            out_send.at[which, chunk, mask - 1], out_recv.at[which, chunk, mask - 1],
            base + partner_of(member, mask),
        )

    def hand_out(chunk):
        for mask in (2, 3, 1):
            for which in range(2):
                out_copy(which, chunk, mask).start()
        for source, target in results:
            target[:, out_columns(chunk)] = source[pl.ds(0, own_units), columns(chunk)]

    for chunk in range(CHUNKS):
        for which in range(2):
            for mask in (2, 3, 1):
                state_copy(which, chunk, mask).start()
    for chunk in range(CHUNKS):
        forward(0, chunk)
    slots = lax.broadcasted_iota(jnp.int32, (tok_tile, hidden.shape[0]), 1)
    for k in range(top_count):

        @pl.loop(0, GROUP)
        def _(tile):
            span = pl.ds(pl.multiple_of(tile * tok_tile, tok_tile), tok_tile)
            picks[k, span] = jnp.where(dest[k, span] == slots, 1.0, 0.0).astype(bf16)

    @pl.loop(0, hidden.shape[0] // block)
    def _(tile):
        span = pl.ds(pl.multiple_of(tile * block, block), block)
        slot = lax.broadcasted_iota(jnp.int32, (block, dest_t.shape[1]), 0) + tile * block
        picks_t[span] = jnp.where(dest_t[...] == slot, 1.0, 0.0).astype(bf16)

    for source, target in states:
        target[pl.ds(0, source.shape[0])] = source[
            :, pl.ds(pl.multiple_of(member * width, 128), width)
        ]
    for step in range(2):
        for chunk in range(CHUNKS):
            residuals(step, chunk)
        for chunk in range(CHUNKS):
            update(step, chunk)
            if step == 0:
                forward(1, chunk)
            else:
                hand_out(chunk)
    for chunk in range(CHUNKS):
        for which in range(2):
            for mask in range(1, GROUP):
                out_copy(which, chunk, mask).wait()
    for phase in range(4):
        source, target = ((sum_out, sum_in), (grad_out, grad_in))[phase % 2]
        for chunk in range(CHUNKS):
            for d in range(1, groups):
                copy_to(source, target, phase, chunk, d).wait_send()


def refit(groups, block, hidden, dest, dest_t, weights, goal, master, first, second):
    bf16, f32 = jnp.bfloat16, jnp.float32
    units, width = master.shape
    rows = hidden.shape[0]
    travel = pltpu.VMEM((2, CHUNKS, rows, width // CHUNKS), bf16)
    state = pltpu.VMEM((units, width), f32)
    sems = pltpu.SemaphoreType.DMA((4, CHUNKS, groups - 1))
    spec = pl.BlockSpec(memory_space=pltpu.VMEM)
    return pl.pallas_call(
        functools.partial(rounds_kernel, groups, block),
        out_shape=[jax.ShapeDtypeStruct(first.shape, bf16)] * 2,
        in_specs=[spec] * 8,
        out_specs=[spec] * 2,
        scratch_shapes=[
            pltpu.VMEM((units, width), bf16), pltpu.VMEM((units, width), bf16),
            pltpu.VMEM((dest.shape[0], dest.shape[1], rows), bf16),
            pltpu.VMEM((rows, dest_t.shape[1]), bf16),
            travel, travel, travel, travel,
            pltpu.VMEM((dest_t.shape[1], width // CHUNKS), bf16),
            pltpu.VMEM((units, width), bf16),
            state, state, state, state, state,
            sems, sems,
            *[pltpu.SemaphoreType.DMA((2, CHUNKS, 3))] * 4,
        ],
        compiler_params=pltpu.CompilerParams(
            collective_id=0, has_side_effects=True, vmem_limit_bytes=60 * 2**20
        ),
    )(hidden, dest, dest_t, weights, goal, master, first, second)


def shards(tokens, targets, routes, gate_ints, expert_home, gate_up, down_master, moment1, moment2):
    devices = lax.axis_size("expert")
    member = lax.axis_index("expert") % GROUP
    tok_rows, top_count = routes.shape
    feat_width = tokens.shape[1]
    width = feat_width // GROUP
    groups = devices // GROUP
    experts = expert_home.shape[0]
    capacity = (5 * tok_rows * top_count * GROUP + 4 * devices - 1) // (4 * devices)
    capacity = -(-capacity // 16) * 16
    slot_rows = groups * capacity
    bf16, f32 = jnp.bfloat16, jnp.float32

    flat_ids = routes.reshape(-1)
    onehot = (flat_ids[:, None] == jnp.arange(experts, dtype=jnp.int32)[None, :]).astype(jnp.int32)
    slot_rank = jnp.sum((jnp.cumsum(onehot, axis=0) - onehot) * onehot, axis=1)
    slot_home = jnp.sum(onehot * expert_home[None, :], axis=1)
    slot_dest = (slot_home * capacity + slot_rank).reshape(tok_rows, top_count)

    row_ids = jnp.arange(slot_rows, dtype=jnp.int32)
    pick_own = jnp.zeros((slot_rows, tok_rows), jnp.bool_)
    for k in range(top_count):
        pick_own = pick_own | (row_ids[:, None] == slot_dest[:, k][None, :])
    outgoing = jnp.dot(
        pick_own.astype(bf16), tokens, preferred_element_type=f32
    ).astype(bf16)

    plan = member_gather(
        jnp.stack([slot_dest.T, gate_ints.T], axis=1)[None], 0
    )
    all_dest, all_gates = plan[:, :, 0], plan[:, :, 1]
    block = GROUP * capacity
    rows = groups * block
    offsets = (jnp.arange(GROUP, dtype=jnp.int32) * capacity)[:, None, None]
    all_dest = all_dest // capacity * block + all_dest % capacity + offsets
    by_choice = all_dest.transpose(1, 0, 2).reshape(top_count, GROUP * tok_rows)
    weights = all_gates.transpose(1, 0, 2).reshape(top_count, GROUP * tok_rows, 1)
    weights = weights.astype(f32) / 4096.0

    hidden, master, goal = dispatch(
        groups, capacity, outgoing, gate_up, down_master.astype(bf16), targets
    )
    moved, moment_one = refit(
        groups, block, hidden, by_choice[:, :, None], by_choice.reshape(1, -1), weights, goal,
        master, moment1, moment2,
    )
    return moved.astype(f32), moment_one.astype(f32)


def solution(mesh):
    in_specs = (
        P("expert", None),
        P("expert", None),
        P(("cand", "expert"), None),
        P(("cand", "expert"), None),
        P("cand"),
        P(None, ("cand", "expert"), None),
        P(("cand", "expert"), None),
        P(("cand", "expert"), None),
        P(("cand", "expert"), None),
    )
    out_specs = (P(("cand", "expert"), None), P(("cand", "expert"), None))
    return jax.shard_map(shards, mesh=mesh, in_specs=in_specs, out_specs=out_specs, check_vma=False)
```
